32 devices in a mesh: ep: 16 (over z, y, core), rep: 2 (over x).
Axes of the slice: x: 2, y: 2, z: 4, core: 2. Of those that a mesh axis runs over, the one named last changes fastest.
Arguments:
- out_grad: bfloat16 [4096, 2048], P(('ep', 'rep')), may hold values from -6 to 6
- hidden: bfloat16 [4096, 8, 768], P(('ep', 'rep')), may hold values from -6 to 6
- expert_ids: int32 [4096, 8], P(('ep', 'rep')), may hold values from 0 to 15, all different within a row; in each aligned block of 128 rows (0 to 127, 128 to 255, ...) at most 72 rows name the same one
- gates: float32 [4096, 8], P(('ep', 'rep')), may hold values from 0.02 to 0.5
- weights: bfloat16 [16, 768, 2048], P('ep', 'rep'), may hold values from -0.125 to 0.125
- row_moment: float32 [16, 768], P('ep', 'rep'), may hold values from 16 to 1024
- col_moment: float32 [16, 2, 2048], P('ep', 'rep'), may hold values from 16 to 1024
Outputs:
- hidden_grad: bfloat16 [4096, 8, 768], P(('ep', 'rep'))
- update: bfloat16 [16, 768, 2048], P('ep', 'rep')
- row_new: float32 [16, 768], P('ep', 'rep')
- col_new: float32 [16, 2, 2048], P('ep', 'rep')
The draws below stay inside these ranges and needn't reach their ends.
Inputs may be any that keep to these rules, and one draw needn't show every extreme that they name: `expert_ids`: the 8 experts of a token are distinct. Among the tokens of one device no expert is chosen more than 72 times, and in every draw some device reaches 72 for some expert.
All inputs are finite; a program needn't handle non-finite values.
Results may differ from the reference program's by a relative error of at most 0.014.
Values may be sent and summed in bfloat16 or wider, within the bound.
A program may use at most 128 MiB of HBM per device.

```python
import math
import jax
import jax.numpy as jnp
import numpy as np
from jax import lax

D = 2048
FF = 768
TOP = 8
TOK_DEV = 128
EXPERTS = 16
CAP = 72
BLK = 384
TOKENS = 4096
N_EP = 16
N_REP = 2


def block_levels(stream_key, extent, cuts, smallest, largest):
    loudness = 1.0
    for position, parts in cuts:
        steps = jax.random.uniform(jax.random.fold_in(jax.random.fold_in(stream_key, 6), position), (parts,), jnp.float32, smallest / len(cuts), largest / len(cuts))
        loudness = loudness * jnp.repeat(jnp.exp(steps), extent[position] // parts).reshape((-1,) + (1,) * (len(extent) - 1 - position))
    return loudness


def routed_block(rng, own, number, rows, number_of, top, bound, lean):
    ranking = jax.random.permutation(rng, number_of)
    packed, usual = portions_of(number_of, rows * top, bound, lean, True), portions_of(number_of, rows * top, bound, lean, False)
    places = jnp.arange(number_of)

    def named(sizes, offset_by):
        used = int((sizes > 0).sum())
        fixed = max(1, used // 4)
        shifted = fixed + (places - fixed + offset_by * (used - fixed)) % max(1, number_of - fixed)
        return jnp.zeros((number_of,), jnp.int32).at[ranking[jnp.where(places < fixed, places, shifted)]].set(jnp.asarray(sizes, jnp.int32))

    sizes = jnp.where(number % 4 == 0, named(packed, number // 4), named(usual, number - number // 4 - 1))
    mixed = jax.random.permutation(jax.random.fold_in(own, 3), number_of)
    donor, taker = mixed[0:number_of // 2 * 2:2], mixed[1:number_of // 2 * 2:2]
    margin = jnp.minimum(sizes[donor] - 1, bound - sizes[taker]) // 2
    margin = jnp.where((donor == ranking[0]) | (taker == ranking[0]) | (sizes[taker] == 0), 0, jnp.maximum(margin, 0))
    shifted = jax.random.randint(jax.random.fold_in(own, 4), (number_of // 2,), 0, 1 << 20) % (margin + 1)
    sizes = sizes.at[donor].add(-shifted).at[taker].add(shifted)
    members = jnp.searchsorted(jnp.cumsum(sizes), jnp.arange(rows * top), side="right").astype(jnp.int32)
    grid = members.reshape(top, rows).T
    grid = grid[jax.random.permutation(jax.random.fold_in(own, 1), rows)]
    offset_by = jax.random.randint(jax.random.fold_in(own, 2), (rows, 1), 0, top)
    return jnp.take_along_axis(grid, (jnp.arange(top)[None, :] + offset_by) % top, axis=1)


def portions_of(number_of, total, bound, skew, full):
    loads = [(1 << 20) // math.isqrt(rank ** skew) + 1 for rank in range(1, number_of + 1)]
    largest = bound if full else min(bound, max(-(-total // number_of), total * loads[0] // sum(loads)))
    least = 1 if total - largest >= number_of - 1 else 0
    holding, rest = [largest] + [least] * (number_of - 1), total - largest - least * (number_of - 1)
    while rest > 0:
        candidates = [i for i in range(1, number_of) if holding[i] < largest] or [i for i in range(1, number_of) if holding[i] < bound]
        pool, budget = sum([loads[i] for i in candidates]), rest
        for i in candidates:
            extra = min(bound - holding[i], max(1, budget * loads[i] // pool), rest)
            holding[i] = holding[i] + extra
            rest = rest - extra
    return np.array(holding)


def gaussian(key, extent, width, bound, pieces=(), held_as=jnp.bfloat16):
    loudness = block_levels(key, extent, pieces, -0.22, 0.18) if pieces else 1.0
    array = jax.random.normal(key, extent, jnp.float32) * width * loudness
    return jnp.minimum(jnp.maximum(array, -bound), bound).astype(held_as)


def setup_inputs(seed: int = 0) -> dict:
    splits = jax.random.split(jax.random.key(seed), 8)
    out_grad = gaussian(splits[0], (TOKENS, D), 1.0, 6.0, ((0, 32),))
    hidden = gaussian(splits[1], (TOKENS, TOP, FF), 1.0, 6.0, ((0, 32),))
    expert_ids_keys = jax.random.split(jax.random.fold_in(splits[2], 1), TOKENS // TOK_DEV)
    expert_ids_turns = jax.random.permutation(jax.random.fold_in(splits[2], 3), TOKENS // TOK_DEV)
    expert_ids = jax.vmap(lambda own, number: routed_block(jax.random.fold_in(splits[2], 2), own, number, TOK_DEV, EXPERTS, TOP, CAP, 1))(expert_ids_keys, expert_ids_turns).reshape((TOKENS, TOP))
    gates = jnp.clip(jnp.exp(math.log(0.5) - 3.218876 * jax.random.uniform(splits[3], (TOKENS, TOP), jnp.float32) ** block_levels(splits[3], (TOKENS, TOP), ((0, 32),), -0.2, 0.2)), 0.02, 0.5)
    weights = gaussian(splits[4], (EXPERTS, FF, D), D ** -0.5, 0.125, ((0, 16), (1, 2)))
    row_moment = jnp.clip(jnp.exp(math.log(1024.0) - 4.158883 * jax.random.uniform(splits[5], (EXPERTS, FF), jnp.float32) ** block_levels(splits[5], (EXPERTS, FF), ((0, 16), (1, 2)), -0.2, 0.2)), 16.0, 1024.0)
    col_moment = jnp.clip(jnp.exp(math.log(1024.0) - 4.158883 * jax.random.uniform(splits[6], (EXPERTS, N_REP, D), jnp.float32) ** block_levels(splits[6], (EXPERTS, N_REP, D), ((0, 16), (1, 2)), -0.2, 0.2)), 16.0, 1024.0)
    return dict(out_grad=out_grad, hidden=hidden, expert_ids=expert_ids, gates=gates, weights=weights, row_moment=row_moment, col_moment=col_moment)


decay_rate = 0.9
epsilon = 1e-06

def reference(out_grad, hidden, expert_ids, gates, weights, row_moment, col_moment):
    routes = TOKENS * TOP
    flat_ids = expert_ids.reshape(routes)
    route_index = jnp.arange(routes, dtype=jnp.int32)
    replica_of = route_index // (TOP * TOK_DEV) % N_REP
    flat_hidden = hidden.reshape(routes, FF)
    flat_gates = gates.reshape(routes)
    limit = N_EP * CAP

    def one_expert(expert):
        matrix = weights[expert]
        gradient = jnp.zeros((FF, D), jnp.float32)
        picked = []
        produced = []
        for replica in range(N_REP):
            chosen = (flat_ids == expert) & (replica_of == replica)
            index = jnp.nonzero(chosen, size=limit, fill_value=routes)[0].astype(jnp.int32)
            valid = index < routes
            safe = jnp.minimum(index, routes - 1)
            token = safe // TOP
            factor = jnp.where(valid, flat_gates[safe], jnp.zeros_like(flat_gates[safe]))
            scaled = (factor[:, None] * out_grad[token].astype(jnp.float32)).astype(jnp.bfloat16)
            rows = flat_hidden[safe]
            term = jnp.dot(rows.T, scaled, preferred_element_type=jnp.float32)
            term = lax.optimization_barrier(term.astype(jnp.bfloat16)).astype(jnp.float32)
            gradient = gradient + term
            produced.append(jnp.dot(scaled, matrix.T, preferred_element_type=jnp.float32).astype(jnp.bfloat16))
            picked.append(index)
        return (gradient, jnp.stack(picked), jnp.stack(produced))
    gradients, picked, produced = lax.map(one_expert, jnp.arange(EXPERTS, dtype=jnp.int32))
    hidden_grad = jnp.zeros((routes, FF), jnp.bfloat16).at[picked.reshape(-1)].set(produced.reshape(-1, FF), mode='drop')
    hidden_grad = hidden_grad.reshape(TOKENS, TOP, FF)
    blocks = gradients.reshape(EXPERTS, N_REP, BLK, D)
    squares = blocks * blocks
    row_new = decay_rate * row_moment.reshape(EXPERTS, N_REP, BLK) + (1.0 - decay_rate) * (lax.optimization_barrier(jnp.mean(squares, axis=3)) + epsilon)
    col_new = decay_rate * col_moment + (1.0 - decay_rate) * (lax.optimization_barrier(jnp.mean(squares, axis=2)) + epsilon)
    second = row_new[:, :, :, None] * col_new[:, :, None, :] / lax.optimization_barrier(jnp.mean(row_new, axis=2))[:, :, None, None]
    update = (blocks * lax.rsqrt(second)).astype(jnp.bfloat16).reshape(EXPERTS, FF, D)
    return (hidden_grad, update, row_new.reshape(EXPERTS, FF), col_new)
```

```python
import jax
import jax.numpy as jnp
from jax import lax
from jax.sharding import PartitionSpec as P

decay_rate = 0.9
epsilon = 1e-06


def local(out_grad, hidden, expert_ids, gates, weights, row_moment, col_moment):
    tok_rows, route_count = expert_ids.shape
    inner = hidden.shape[2]
    experts = lax.axis_size("ep")
    capacity = max(2, tok_rows * route_count * 9 // (8 * experts))
    routes = tok_rows * route_count
    slots = experts * capacity

    gathered = lax.all_gather(out_grad, "ep", axis=0, tiled=False)
    weight = lax.all_gather(weights[0], "rep", axis=0, tiled=True)

    hit = expert_ids[:, :, None] == jnp.arange(experts, dtype=jnp.int32)
    chosen = jnp.any(hit, axis=1)
    before = jnp.tril(jnp.ones((tok_rows, tok_rows), jnp.bfloat16), -1)
    rank = jnp.dot(
        before, chosen.astype(jnp.bfloat16), preferred_element_type=jnp.float32
    ).astype(jnp.int32)
    place = jnp.where(chosen, rank, -1).T
    place_in = lax.all_to_all(place, "ep", split_axis=0, concat_axis=0, tiled=True)

    rank_own = jnp.sum(jnp.where(hit, rank[:, None, :], 0), axis=2)
    position = (expert_ids * capacity + rank_own).reshape(routes)

    gated = (
        (gates[:, :, None] * hidden.astype(jnp.float32))
        .astype(jnp.bfloat16)
        .reshape(routes, inner)
    )
    send_hidden = jnp.zeros((slots, inner), jnp.bfloat16).at[position].set(gated)
    recv_hidden = lax.all_to_all(send_hidden, "ep", split_axis=0, concat_axis=0, tiled=True)

    pick = (place_in[:, None, :] == jnp.arange(capacity, dtype=jnp.int32)[None, :, None]).astype(
        jnp.bfloat16
    )
    rows = (
        jnp.einsum("sjt,std->sjd", pick, gathered, preferred_element_type=jnp.float32)
        .astype(jnp.bfloat16)
        .reshape(slots, -1)
    )
    input_grad = lax.dot_general(
        rows, weight, (((1,), (1,)), ((), ())), preferred_element_type=jnp.float32
    ).astype(jnp.bfloat16)
    returned = lax.all_to_all(input_grad, "ep", split_axis=0, concat_axis=0, tiled=True)
    term = lax.dot_general(
        recv_hidden, rows, (((0,), (0,)), ((), ())), preferred_element_type=jnp.float32
    )
    gradient = lax.psum_scatter(
        term.astype(jnp.bfloat16), "rep", scatter_dimension=0, tiled=True
    ).astype(jnp.float32)
    hidden_grad = (
        gates[:, :, None]
        * returned[position].reshape(tok_rows, route_count, inner).astype(jnp.float32)
    ).astype(jnp.bfloat16)
    squares = gradient * gradient
    row_new = decay_rate * row_moment[0] + (1.0 - decay_rate) * (
        jnp.mean(squares, axis=1) + epsilon
    )
    col_new = decay_rate * col_moment[0, 0] + (1.0 - decay_rate) * (
        jnp.mean(squares, axis=0) + epsilon
    )
    second = row_new[:, None] * col_new[None, :] / jnp.mean(row_new)
    update = (gradient * lax.rsqrt(second)).astype(jnp.bfloat16)
    return (hidden_grad, update[None], row_new[None], col_new[None, None])


def solution(mesh):
    return jax.shard_map(
        local,
        mesh=mesh,
        in_specs=(
            P(("ep", "rep"), None),
            P(("ep", "rep"), None, None),
            P(("ep", "rep"), None),
            P(("ep", "rep"), None),
            P("ep", "rep", None),
            P("ep", "rep"),
            P("ep", "rep", None),
        ),
        out_specs=(
            P(("ep", "rep"), None, None),
            P("ep", "rep", None),
            P("ep", "rep"),
            P("ep", "rep", None),
        ),
        check_vma=False,
    )
```

```python
import functools

import jax
import jax.numpy as jnp
from jax import lax
from jax.experimental import pallas as pl
from jax.experimental.pallas import tpu as pltpu
from jax.sharding import PartitionSpec as P

decay_rate = 0.9
epsilon = 1e-06
MESH = pl.DeviceIdType.MESH


def up_to(value, step):
    return -(-value // step) * step


def kernel(
    dims,
    og_ref,
    gated_ref,
    slot_ref,
    place_ref,
    w_ref,
    rowm_ref,
    colm_ref,
    returned_ref,
    update_ref,
    rown_ref,
    coln_ref,
    og_all,
    place_all,
    hsend,
    hrecv,
    rows,
    igbuf,
    wfull,
    parts,
    grad,
    og_recv,
    up_sem,
    down_sem,
    y_sem,
    core_sem,
    pl_send,
    pl_recv,
    h_send,
    h_recv,
    r_send,
    r_recv,
    w_send,
    w_recv,
    g_send,
    g_recv,
):
    n_ep, n_rep, outer, sent, cap, chunks = dims
    tok, width = og_ref.shape
    inner = gated_ref.shape[1]
    own_rows = inner // n_rep
    wide = width // chunks
    term = wfull
    me = lax.axis_index("ep")
    rep = lax.axis_index("rep")
    z, y, c = me // 4, (me // 2) % 2, me % 2
    y_dev = z * 4 + (1 - y) * 2 + c
    c_dev = z * 4 + y * 2 + (1 - c)
    way = 1 - 2 * (z // (outer // 2))

    og_all[me] = og_ref[...]
    wfull[rep] = w_ref[...]
    place_all[me] = place_ref[me]
    hrecv[...] = jnp.zeros_like(hrecv)

    barrier = pltpu.get_barrier_semaphore()
    for d in range(1, n_ep):
        pl.semaphore_signal(
            barrier, inc=1, device_id={"ep": lax.rem(me + d, n_ep)}, device_id_type=MESH
        )
    for d in range(1, n_rep):
        pl.semaphore_signal(
            barrier, inc=1, device_id={"rep": lax.rem(rep + d, n_rep)}, device_id_type=MESH
        )
    pl.semaphore_wait(barrier, n_ep - 1 + n_rep - 1)

    def remote(src, dst, send, recv, **where):
        return pltpu.make_async_remote_copy(
            src_ref=src, dst_ref=dst, send_sem=send, recv_sem=recv,
            device_id=where, device_id_type=MESH,
        )

    def og_copy(block, send, to, own):
        src = og_ref if own else og_all.at[block]
        return remote(src, og_all.at[block], send, og_recv.at[block], ep=to)

    def og_wait(block):
        remote(og_all.at[block], og_all.at[block], up_sem.at[0], og_recv.at[block], ep=me).wait_recv()

    def fan(zs, k, act):
        block = zs * 4 + y * 2 + c
        act(og_copy(block, y_sem.at[zs], y_dev, k == 0))
        act(og_copy(block, core_sem.at[zs * 2], c_dev, k == 0))

    def rise(zs, k, act):
        block = zs * 4 + y * 2 + c

        @pl.when(z + 1 < outer)
        def _():
            act(og_copy(block, up_sem.at[zs], me + 4, k == 0))

    def sink(zs, k, act):
        block = zs * 4 + y * 2 + c

        @pl.when(z > 0)
        def _():
            act(og_copy(block, down_sem.at[zs], me - 4, k == 0))

    def cross(zs, act):
        block = zs * 4 + (1 - y) * 2 + c
        act(og_copy(block, core_sem.at[zs * 2 + 1], c_dev, False))

    start = lambda copy: copy.start()
    finish = lambda copy: copy.wait_send()

    def own_sends(act):
        rise(z, 0, act)
        sink(z, 0, act)
        fan(z, 0, act)

    def forward(k, act, arrive):
        low, high = z - k, z + k

        @pl.when(low >= 0)
        def _():
            if arrive:
                og_wait(low * 4 + y * 2 + c)
            rise(low, k, act)
            fan(low, k, act)

        @pl.when(high < outer)
        def _():
            if arrive:
                og_wait(high * 4 + y * 2 + c)
            sink(high, k, act)
            fan(high, k, act)

    def crossing(k, act, arrive):
        for zs, ok in ((z - k, z - k >= 0), (z + k, z + k < outer))[: 1 if k == 0 else 2]:

            @pl.when(ok)
            def _():
                if arrive:
                    og_wait(zs * 4 + (1 - y) * 2 + c)
                cross(zs, act)

    own_sends(start)
    w_copies = []
    for d in range(1, n_rep):
        q = lax.rem(rep + d, n_rep)
        w_copies.append(remote(w_ref, wfull.at[rep], w_send.at[d], w_recv.at[rep], rep=q))
        w_copies[-1].start()

    def place_copy(d):
        e = lax.rem(me + d, n_ep)
        return remote(place_ref.at[e], place_all.at[me], pl_send.at[d], pl_recv.at[me], ep=e)

    @pl.loop(1, n_ep)
    def _(d):
        place_copy(d).start()

    def h_copy(e):
        return remote(hsend.at[e, pl.ds(0, sent)], hrecv.at[me, pl.ds(0, sent)], h_send.at[e], h_recv.at[me], ep=e)

    def r_copy(s):
        return remote(igbuf.at[s, pl.ds(0, sent)], returned_ref.at[me], r_send.at[s], r_recv.at[me], ep=s)

    def plane(k):
        return lax.rem(z + way * k + outer, outer)

    def hidden_group(k):
        first = plane(k) * 4
        ids = lax.broadcasted_iota(jnp.int32, (4 * cap, slot_ref.shape[1]), 0) + first * cap
        pick = jnp.where(ids == slot_ref[...], 1.0, 0.0).astype(jnp.bfloat16)
        got = jnp.dot(pick, gated_ref[...], preferred_element_type=jnp.float32)
        hsend[pl.ds(first, 4)] = got.astype(jnp.bfloat16).reshape(4, cap, inner)

        @pl.loop(0, 4)
        def _(i):
            e = first + i

            @pl.when(e != me)
            def _():
                h_copy(e).start()

            @pl.when(e == me)
            def _():
                hrecv[me] = hsend[me]

    hidden_group(0)
    for k in range(1, outer):
        forward(k, start, True)
        hidden_group(k)
        crossing(k - 1, start, True)
    crossing(outer - 1, start, True)

    for d in range(1, n_rep):
        q = lax.rem(rep + d, n_rep)
        remote(w_ref, wfull.at[q], w_send.at[d], w_recv.at[q], rep=q).wait_recv()

    @pl.loop(1, n_ep)
    def _(d):
        s = lax.rem(me + d, n_ep)
        remote(place_ref.at[s], place_all.at[s], pl_send.at[d], pl_recv.at[s], ep=s).wait_recv()

    @pl.loop(0, outer)
    def _(k):
        first = plane(k) * 4
        og_wait(first + 1 - c)
        og_wait(first + 3 - c)

        @pl.loop(0, 4)
        def _(i):
            s = first + i
            ids = lax.broadcasted_iota(jnp.int32, (cap, tok), 0)
            pick = jnp.where(ids == place_all[s][0:1, :], 1.0, 0.0).astype(jnp.bfloat16)
            got = jnp.dot(pick, og_all[s], preferred_element_type=jnp.float32)
            rows[pl.ds(pl.multiple_of(s * cap, 16), cap), :] = got.astype(jnp.bfloat16)

        here = rows[pl.ds(pl.multiple_of(first * cap, 16), 4 * cap), :]
        back = lax.dot_general(
            here,
            wfull[...].reshape(inner, width),
            (((1,), (1,)), ((), ())),
            preferred_element_type=jnp.float32,
        )
        igbuf[pl.ds(first, 4)] = back.astype(jnp.bfloat16).reshape(4, cap, inner)

        @pl.loop(0, 4)
        def _(i):
            s = first + i

            @pl.when(s != me)
            def _():
                r_copy(s).start()

    own = pltpu.make_async_copy(igbuf.at[me, pl.ds(0, sent)], returned_ref.at[me], r_recv.at[me])
    own.start()

    @pl.loop(1, n_ep)
    def _(d):
        s = lax.rem(me + d, n_ep)
        remote(hsend.at[s, pl.ds(0, sent)], hrecv.at[s, pl.ds(0, sent)], h_send.at[s], h_recv.at[s], ep=s).wait_recv()

    def g_copy(d, j, q, slot):
        cols = pl.ds(j * wide, wide)
        return remote(
            term.at[q, :, cols], parts.at[slot, :, cols],
            g_send.at[d, j], g_recv.at[slot, j], rep=q,
        )

    left = hrecv[...].reshape(n_ep * cap, inner)
    for j in range(chunks):
        cols = pl.ds(j * wide, wide)
        got = lax.dot_general(
            left, rows[:, cols], (((0,), (0,)), ((), ())), preferred_element_type=jnp.float32
        )
        term[:, :, cols] = got.astype(jnp.bfloat16).reshape(n_rep, own_rows, wide)
        for d in range(1, n_rep):
            g_copy(d, j, lax.rem(rep + d, n_rep), rep).start()

    total = jnp.zeros((own_rows, 1), jnp.float32)
    for j in range(chunks):
        cols = pl.ds(j * wide, wide)
        part = term[rep, :, cols].astype(jnp.float32)
        for d in range(1, n_rep):
            q = lax.rem(rep + d, n_rep)
            g_copy(d, j, q, q).wait_recv()
            part = part + parts[q, :, cols].astype(jnp.float32)
        grad[:, cols] = part
        square = part * part
        total = total + jnp.sum(square, axis=1, keepdims=True)
        coln_ref[:, cols] = decay_rate * colm_ref[:, cols] + (1.0 - decay_rate) * (
            jnp.sum(square, axis=0, keepdims=True) / own_rows + epsilon
        )
    row_new = decay_rate * rowm_ref[...] + (1.0 - decay_rate) * (total / width + epsilon)
    rown_ref[...] = row_new
    mean = jnp.sum(row_new, axis=0, keepdims=True) / own_rows
    for j in range(chunks):
        cols = pl.ds(j * wide, wide)
        second = row_new * coln_ref[:, cols] / mean
        update_ref[:, cols] = (grad[:, cols] * lax.rsqrt(second)).astype(jnp.bfloat16)

    own.wait()

    @pl.loop(1, n_ep)
    def _(d):
        s = lax.rem(me + d, n_ep)
        place_copy(d).wait_send()
        h_copy(s).wait_send()
        r_copy(s).wait_send()
        remote(igbuf.at[s, pl.ds(0, sent)], returned_ref.at[s], r_send.at[s], r_recv.at[s], ep=s).wait_recv()

    own_sends(finish)
    for k in range(1, outer):
        forward(k, finish, False)
        crossing(k - 1, finish, False)
    crossing(outer - 1, finish, False)
    for copy in w_copies:
        copy.wait_send()
    for j in range(chunks):
        for d in range(1, n_rep):
            g_copy(d, j, lax.rem(rep + d, n_rep), rep).wait_send()


def local(out_grad, hidden, expert_ids, gates, weights, row_moment, col_moment):
    tok, top = expert_ids.shape
    width = out_grad.shape[1]
    inner = hidden.shape[2]
    n_ep, n_rep = lax.axis_size("ep"), lax.axis_size("rep")
    capacity = max(2, tok * top * 9 // (8 * n_ep))
    sent, cap = up_to(capacity, 8), up_to(capacity, 16)
    outer = n_ep // 4
    own_rows = inner // n_rep
    routes = tok * top
    chunks = 4

    hit = expert_ids[:, :, None] == jnp.arange(n_ep, dtype=jnp.int32)
    chosen = jnp.any(hit, axis=1)
    before = jnp.tril(jnp.ones((tok, tok), jnp.bfloat16), -1)
    rank = jnp.dot(
        before, chosen.astype(jnp.bfloat16), preferred_element_type=jnp.float32
    ).astype(jnp.int32)
    place = jnp.where(chosen, rank, -1).T
    place = jnp.broadcast_to(place[:, None, :], (n_ep, 8, tok))
    rank_own = jnp.sum(jnp.where(hit, rank[:, None, :], 0), axis=2)
    slot = (expert_ids * cap + rank_own).reshape(1, routes)
    position = (expert_ids * sent + rank_own).reshape(routes)
    gated = (
        (gates[:, :, None] * hidden.astype(jnp.float32)).astype(jnp.bfloat16).reshape(routes, inner)
    )

    vmem = pl.BlockSpec(memory_space=pltpu.VMEM)
    anywhere = pl.BlockSpec(memory_space=pl.ANY)
    dma = pltpu.SemaphoreType.DMA
    returned, update, row_new, col_new = pl.pallas_call(
        functools.partial(kernel, (n_ep, n_rep, outer, sent, cap, chunks)),
        out_shape=(
            jax.ShapeDtypeStruct((n_ep, sent, inner), jnp.bfloat16),
            jax.ShapeDtypeStruct((own_rows, width), jnp.bfloat16),
            jax.ShapeDtypeStruct((own_rows, 1), jnp.float32),
            jax.ShapeDtypeStruct((1, width), jnp.float32),
        ),
        in_specs=[vmem] * 7,
        out_specs=(anywhere, vmem, vmem, vmem),
        scratch_shapes=[
            pltpu.VMEM((n_ep, tok, width), jnp.bfloat16),
            pltpu.VMEM((n_ep, 8, tok), jnp.int32),
            pltpu.VMEM((n_ep, cap, inner), jnp.bfloat16),
            pltpu.VMEM((n_ep, cap, inner), jnp.bfloat16),
            pltpu.VMEM((n_ep * cap, width), jnp.bfloat16),
            pltpu.VMEM((n_ep, cap, inner), jnp.bfloat16),
            pltpu.VMEM((n_rep, own_rows, width), jnp.bfloat16),
            pltpu.VMEM((n_rep, own_rows, width), jnp.bfloat16),
            pltpu.VMEM((own_rows, width), jnp.float32),
            dma((n_ep,)),
            dma((outer,)),
            dma((outer,)),
            dma((outer,)),
            dma((2 * outer,)),
            dma((n_ep,)),
            dma((n_ep,)),
            dma((n_ep,)),
            dma((n_ep,)),
            dma((n_ep,)),
            dma((n_ep,)),
            dma((n_rep,)),
            dma((n_rep,)),
            dma((n_rep, chunks)),
            dma((n_rep, chunks)),
        ],
        compiler_params=pltpu.CompilerParams(
            collective_id=0, has_side_effects=True, vmem_limit_bytes=67043328
        ),
    )(
        out_grad,
        gated,
        slot,
        place,
        weights[0],
        row_moment.reshape(own_rows, 1),
        col_moment.reshape(1, width),
    )

    back = returned.reshape(n_ep * sent, inner)[position].reshape(tok, top, inner)
    hidden_grad = (gates[:, :, None] * back.astype(jnp.float32)).astype(jnp.bfloat16)
    return (
        hidden_grad,
        update[None],
        row_new.reshape(1, own_rows),
        col_new.reshape(1, 1, width),
    )


def solution(mesh):
    return jax.shard_map(
        local,
        mesh=mesh,
        in_specs=(
            P(("ep", "rep"), None),
            P(("ep", "rep"), None, None),
            P(("ep", "rep"), None),
            P(("ep", "rep"), None),
            P("ep", "rep", None),
            P("ep", "rep"),
            P("ep", "rep", None),
        ),
        out_specs=(
            P(("ep", "rep"), None, None),
            P("ep", "rep", None),
            P("ep", "rep"),
            P("ep", "rep", None),
        ),
        check_vma=False,
    )
```

```python
import functools

import jax
import jax.numpy as jnp
from jax import lax
from jax.experimental import pallas as pl
from jax.experimental.pallas import tpu as pltpu
from jax.sharding import PartitionSpec as P

decay_rate = 0.9
epsilon = 1e-06
MESH = pl.DeviceIdType.MESH


def up_to(value, step):
    return -(-value // step) * step


def kernel(
    dims,
    og_ref,
    hidden_ref,
    ids_ref,
    gates_ref,
    w_ref,
    rowm_ref,
    colm_ref,
    returned_ref,
    out_ref,
    update_ref,
    rown_ref,
    coln_ref,
    og_all,
    hid,
    slot,
    table,
    place_all,
    hsend,
    hrecv,
    rows,
    igbuf,
    wfull,
    parts,
    grad,
    og_recv,
    up_sem,
    down_sem,
    y_sem,
    core_sem,
    pl_send,
    pl_recv,
    h_send,
    h_recv,
    r_send,
    r_recv,
    w_send,
    w_recv,
    g_send,
    g_recv,
    l_sem,
):
    n_ep, n_rep, outer, sent, cap, chunks = dims
    tok, width = og_ref.shape
    routes, inner = hidden_ref.shape
    top = routes // tok
    own_rows = inner // n_rep
    wide = width // chunks
    term = wfull
    me = lax.axis_index("ep")
    rep = lax.axis_index("rep")
    z, y, c = me // 4, (me // 2) % 2, me % 2
    y_dev = z * 4 + (1 - y) * 2 + c
    c_dev = z * 4 + y * 2 + (1 - c)
    way = 1 - 2 * (z // (outer // 2))

    barrier = pltpu.get_barrier_semaphore()
    for d in range(1, n_ep):
        pl.semaphore_signal(
            barrier, inc=1, device_id={"ep": lax.rem(me + d, n_ep)}, device_id_type=MESH
        )
    for d in range(1, n_rep):
        pl.semaphore_signal(
            barrier, inc=1, device_id={"rep": lax.rem(rep + d, n_rep)}, device_id_type=MESH
        )
    pl.semaphore_wait(barrier, n_ep - 1 + n_rep - 1)

    def remote(src, dst, send, recv, **where):
        return pltpu.make_async_remote_copy(
            src_ref=src, dst_ref=dst, send_sem=send, recv_sem=recv,
            device_id=where, device_id_type=MESH,
        )

    def og_copy(block, send, to, own):
        src = og_ref if own else og_all.at[block]
        return remote(src, og_all.at[block], send, og_recv.at[block], ep=to)

    def og_wait(block):
        remote(og_all.at[block], og_all.at[block], up_sem.at[0], og_recv.at[block], ep=me).wait_recv()

    def fan(zs, k, act):
        block = zs * 4 + y * 2 + c
        act(og_copy(block, y_sem.at[zs], y_dev, k == 0))
        act(og_copy(block, core_sem.at[zs * 2], c_dev, k == 0))

    def rise(zs, k, act):
        block = zs * 4 + y * 2 + c

        @pl.when(z + 1 < outer)
        def _():
            act(og_copy(block, up_sem.at[zs], me + 4, k == 0))

    def sink(zs, k, act):
        block = zs * 4 + y * 2 + c

        @pl.when(z > 0)
        def _():
            act(og_copy(block, down_sem.at[zs], me - 4, k == 0))

    def cross(zs, act):
        block = zs * 4 + (1 - y) * 2 + c
        act(og_copy(block, core_sem.at[zs * 2 + 1], c_dev, False))

    start = lambda copy: copy.start()
    finish = lambda copy: copy.wait_send()

    def own_sends(act):
        rise(z, 0, act)
        sink(z, 0, act)
        fan(z, 0, act)

    def forward(k, act, arrive):
        low, high = z - k, z + k

        @pl.when(low >= 0)
        def _():
            if arrive:
                og_wait(low * 4 + y * 2 + c)
            rise(low, k, act)
            fan(low, k, act)

        @pl.when(high < outer)
        def _():
            if arrive:
                og_wait(high * 4 + y * 2 + c)
            sink(high, k, act)
            fan(high, k, act)

    def crossing(k, act, arrive):
        for zs, ok in ((z - k, z - k >= 0), (z + k, z + k < outer))[: 1 if k == 0 else 2]:

            @pl.when(ok)
            def _():
                if arrive:
                    og_wait(zs * 4 + (1 - y) * 2 + c)
                cross(zs, act)

    own_sends(start)
    own_og = pltpu.make_async_copy(og_ref, og_all.at[me], l_sem.at[0])
    own_w = pltpu.make_async_copy(w_ref, wfull.at[rep], l_sem.at[1])
    own_hidden = pltpu.make_async_copy(hidden_ref, hid, l_sem.at[2])
    own_hidden.start()
    own_og.start()
    own_w.start()
    w_copies = []
    for d in range(1, n_rep):
        q = lax.rem(rep + d, n_rep)
        w_copies.append(remote(w_ref, wfull.at[rep], w_send.at[d], w_recv.at[rep], rep=q))
        w_copies[-1].start()

    experts = lax.broadcasted_iota(jnp.int32, (tok, up_to(n_ep, 128)), 1)
    chosen = jnp.zeros(experts.shape, jnp.float32)
    gate = jnp.zeros(experts.shape, jnp.float32)
    for k in range(top):
        named = experts == ids_ref[:, k : k + 1]
        chosen = jnp.where(named, 1.0, chosen)
        gate = jnp.where(named, gates_ref[:, k : k + 1], gate)
    row_i = lax.broadcasted_iota(jnp.int32, (tok, tok), 0)
    col_i = lax.broadcasted_iota(jnp.int32, (tok, tok), 1)
    earlier = jnp.where(row_i < col_i, 1.0, 0.0).astype(jnp.bfloat16)
    rank = lax.dot_general(
        chosen.T.astype(jnp.bfloat16), earlier, (((1,), (0,)), ((), ())),
        preferred_element_type=jnp.float32,
    )
    place = jnp.where(chosen.T > 0.5, rank, -1.0)[:n_ep]
    gate = gate.T[:n_ep]
    first_row = lax.broadcasted_iota(jnp.int32, (n_ep, 8, tok), 1) == 0
    table[...] = jnp.where(first_row, place[:, None, :], gate[:, None, :])
    place_all[me] = table[me]
    if cap > sent:
        hrecv[:, sent:, :] = jnp.zeros((n_ep, cap - sent, inner), jnp.bfloat16)

    spread = jnp.where(
        lax.broadcasted_iota(jnp.int32, (tok, routes), 1) // top
        == lax.broadcasted_iota(jnp.int32, (tok, routes), 0), 1.0, 0.0,
    ).astype(jnp.bfloat16)
    named = lax.dot_general(
        ids_ref[...].astype(jnp.float32).astype(jnp.bfloat16), spread, (((0,), (0,)), ((), ())),
        preferred_element_type=jnp.float32,
    )
    turn = lax.broadcasted_iota(jnp.int32, (top, routes), 1) % top
    mine = turn == lax.broadcasted_iota(jnp.int32, (top, routes), 0)
    named = jnp.sum(jnp.where(mine, named, 0.0), axis=0, keepdims=True)
    ranks = jnp.dot(place.astype(jnp.bfloat16), spread, preferred_element_type=jnp.float32)
    number = lax.broadcasted_iota(jnp.int32, (n_ep, routes), 0).astype(jnp.float32)
    slot[...] = jnp.sum(
        jnp.where(named == number, ranks + number * cap, 0.0), axis=0, keepdims=True
    )

    def place_copy(d):
        e = lax.rem(me + d, n_ep)
        return remote(table.at[e], place_all.at[me], pl_send.at[d], pl_recv.at[me], ep=e)

    @pl.loop(1, n_ep)
    def _(d):
        place_copy(d).start()

    def h_copy(e):
        return remote(hsend.at[e, pl.ds(0, sent)], hrecv.at[me, pl.ds(0, sent)], h_send.at[e], h_recv.at[me], ep=e)

    def r_copy(s):
        return remote(igbuf.at[s, pl.ds(0, sent)], returned_ref.at[me], r_send.at[s], r_recv.at[me], ep=s)

    def plane(k):
        return lax.rem(z + way * k + outer, outer)

    def slot_pick(first):
        ids = lax.broadcasted_iota(jnp.int32, (4 * cap, routes), 0) + first * cap
        return jnp.where(ids.astype(jnp.float32) == slot[...], 1.0, 0.0).astype(jnp.bfloat16)

    def hidden_group(k):
        first = plane(k) * 4
        got = jnp.dot(slot_pick(first), hid[...], preferred_element_type=jnp.float32)
        hsend[pl.ds(first, 4)] = got.astype(jnp.bfloat16).reshape(4, cap, inner)

        @pl.loop(0, 4)
        def _(i):
            e = first + i

            @pl.when(e != me)
            def _():
                h_copy(e).start()

            @pl.when(e == me)
            def _():
                hrecv[me] = hsend[me]

    own_hidden.wait()
    hidden_group(0)
    for k in range(1, outer):
        forward(k, start, True)
        hidden_group(k)
        crossing(k - 1, start, True)
    crossing(outer - 1, start, True)

    for d in range(1, n_rep):
        q = lax.rem(rep + d, n_rep)
        remote(w_ref, wfull.at[q], w_send.at[d], w_recv.at[q], rep=q).wait_recv()

    @pl.loop(1, n_ep)
    def _(d):
        s = lax.rem(me + d, n_ep)
        remote(table.at[s], place_all.at[s], pl_send.at[d], pl_recv.at[s], ep=s).wait_recv()

    own_og.wait()
    own_w.wait()

    @pl.loop(0, outer)
    def _(k):
        first = plane(k) * 4
        og_wait(first + 1 - c)
        og_wait(first + 3 - c)

        @pl.loop(0, 4)
        def _(i):
            s = first + i
            info = place_all[s]
            ids = lax.broadcasted_iota(jnp.int32, (cap, tok), 0).astype(jnp.float32)
            pick = jnp.where(ids == info[0:1, :], 1.0, 0.0)
            factor = jnp.sum(pick * info[1:2, :], axis=1, keepdims=True)
            got = factor * jnp.dot(
                pick.astype(jnp.bfloat16), og_all[s], preferred_element_type=jnp.float32
            )
            rows[pl.ds(pl.multiple_of(s * cap, 16), cap), :] = got.astype(jnp.bfloat16)

        here = rows[pl.ds(pl.multiple_of(first * cap, 16), 4 * cap), :]
        back = lax.dot_general(
            here,
            wfull[...].reshape(inner, width),
            (((1,), (1,)), ((), ())),
            preferred_element_type=jnp.float32,
        )
        igbuf[pl.ds(first, 4)] = back.astype(jnp.bfloat16).reshape(4, cap, inner)

        @pl.loop(0, 4)
        def _(i):
            s = first + i

            @pl.when(s != me)
            def _():
                r_copy(s).start()

    own = pltpu.make_async_copy(igbuf.at[me, pl.ds(0, sent)], returned_ref.at[me], r_recv.at[me])
    own.start()

    @pl.loop(1, n_ep)
    def _(d):
        s = lax.rem(me + d, n_ep)
        remote(hsend.at[s, pl.ds(0, sent)], hrecv.at[s, pl.ds(0, sent)], h_send.at[s], h_recv.at[s], ep=s).wait_recv()

    def g_copy(d, j, q, slot):
        cols = pl.ds(j * wide, wide)
        return remote(
            term.at[q, :, cols], parts.at[slot, :, cols],
            g_send.at[d, j], g_recv.at[slot, j], rep=q,
        )

    left = hrecv[...].reshape(n_ep * cap, inner)
    for j in range(chunks):
        cols = pl.ds(j * wide, wide)
        got = lax.dot_general(
            left, rows[:, cols], (((0,), (0,)), ((), ())), preferred_element_type=jnp.float32
        )
        term[:, :, cols] = got.astype(jnp.bfloat16).reshape(n_rep, own_rows, wide)
        for d in range(1, n_rep):
            g_copy(d, j, lax.rem(rep + d, n_rep), rep).start()

    def back_copy(first):
        return pltpu.make_async_copy(
            returned_ref.at[pl.ds(first, 4)], hsend.at[pl.ds(first, 4), pl.ds(0, sent)], l_sem.at[0]
        )

    def collect(k):
        first = plane(k) * 4

        @pl.loop(0, 4)
        def _(i):
            s = first + i

            @pl.when(s != me)
            def _():
                h_copy(s).wait_send()
                remote(
                    igbuf.at[s, pl.ds(0, sent)], returned_ref.at[s], r_send.at[s], r_recv.at[s], ep=s
                ).wait_recv()

        back_copy(first).start()
        back_copy(first).wait()
        got = lax.dot_general(
            slot_pick(first),
            hsend[pl.ds(first, 4)].reshape(4 * cap, inner),
            (((0,), (0,)), ((), ())),
            preferred_element_type=jnp.float32,
        ).astype(jnp.bfloat16)
        out_ref[...] = got if k == 0 else out_ref[...] + got

    own.wait()
    for k in range(outer - 1):
        collect(k)

    total = jnp.zeros((own_rows, 1), jnp.float32)
    for j in range(chunks):
        cols = pl.ds(j * wide, wide)
        part = term[rep, :, cols].astype(jnp.float32)
        for d in range(1, n_rep):
            q = lax.rem(rep + d, n_rep)
            g_copy(d, j, q, q).wait_recv()
            part = part + parts[q, :, cols].astype(jnp.float32)
        grad[:, cols] = part
        square = part * part
        total = total + jnp.sum(square, axis=1, keepdims=True)
        coln_ref[:, cols] = decay_rate * colm_ref[:, cols] + (1.0 - decay_rate) * (
            jnp.sum(square, axis=0, keepdims=True) / own_rows + epsilon
        )
    diagonal = lax.broadcasted_iota(jnp.int32, (own_rows, own_rows), 0) == (
        lax.broadcasted_iota(jnp.int32, (own_rows, own_rows), 1)
    )
    rowm = jnp.sum(jnp.where(diagonal, rowm_ref[...], 0.0), axis=1, keepdims=True)
    row_new = decay_rate * rowm + (1.0 - decay_rate) * (total / width + epsilon)
    rown_ref[...] = jnp.sum(jnp.where(diagonal, row_new, 0.0), axis=0, keepdims=True)
    mean = jnp.sum(row_new, axis=0, keepdims=True) / own_rows
    for j in range(chunks):
        cols = pl.ds(j * wide, wide)
        second = row_new * coln_ref[:, cols] / mean
        update_ref[:, cols] = (grad[:, cols] * lax.rsqrt(second)).astype(jnp.bfloat16)

    collect(outer - 1)

    @pl.loop(1, n_ep)
    def _(d):
        s = lax.rem(me + d, n_ep)
        place_copy(d).wait_send()
        r_copy(s).wait_send()

    own_sends(finish)
    for k in range(1, outer):
        forward(k, finish, False)
        crossing(k - 1, finish, False)
    crossing(outer - 1, finish, False)
    for copy in w_copies:
        copy.wait_send()
    for j in range(chunks):
        for d in range(1, n_rep):
            g_copy(d, j, lax.rem(rep + d, n_rep), rep).wait_send()


def local(out_grad, hidden, expert_ids, gates, weights, row_moment, col_moment):
    tok, top = expert_ids.shape
    width = out_grad.shape[1]
    inner = hidden.shape[2]
    n_ep, n_rep = lax.axis_size("ep"), lax.axis_size("rep")
    capacity = max(2, tok * top * 9 // (8 * n_ep))
    sent, cap = up_to(capacity, 8), up_to(capacity, 16)
    outer = n_ep // 4
    own_rows = inner // n_rep
    routes = tok * top
    chunks = 4

    vmem = pl.BlockSpec(memory_space=pltpu.VMEM)
    anywhere = pl.BlockSpec(memory_space=pl.ANY)
    dma = pltpu.SemaphoreType.DMA
    _, hidden_grad, update, row_new, col_new = pl.pallas_call(
        functools.partial(kernel, (n_ep, n_rep, outer, sent, cap, chunks)),
        out_shape=(
            jax.ShapeDtypeStruct((n_ep, sent, inner), jnp.bfloat16),
            jax.ShapeDtypeStruct((routes, inner), jnp.bfloat16),
            jax.ShapeDtypeStruct((own_rows, width), jnp.bfloat16),
            jax.ShapeDtypeStruct((1, own_rows), jnp.float32),
            jax.ShapeDtypeStruct((1, width), jnp.float32),
        ),
        in_specs=[anywhere, anywhere, vmem, vmem, anywhere, vmem, vmem],
        out_specs=(anywhere, vmem, vmem, vmem, vmem),
        scratch_shapes=[
            pltpu.VMEM((n_ep, tok, width), jnp.bfloat16),
            pltpu.VMEM((routes, inner), jnp.bfloat16),
            pltpu.VMEM((1, routes), jnp.float32),
            pltpu.VMEM((n_ep, 8, tok), jnp.float32),
            pltpu.VMEM((n_ep, 8, tok), jnp.float32),
            pltpu.VMEM((n_ep, cap, inner), jnp.bfloat16),
            pltpu.VMEM((n_ep, cap, inner), jnp.bfloat16),
            pltpu.VMEM((n_ep * cap, width), jnp.bfloat16),
            pltpu.VMEM((n_ep, cap, inner), jnp.bfloat16),
            pltpu.VMEM((n_rep, own_rows, width), jnp.bfloat16),
            pltpu.VMEM((n_rep, own_rows, width), jnp.bfloat16),
            pltpu.VMEM((own_rows, width), jnp.float32),
            dma((n_ep,)),
            dma((outer,)),
            dma((outer,)),
            dma((outer,)),
            dma((2 * outer,)),
            dma((n_ep,)),
            dma((n_ep,)),
            dma((n_ep,)),
            dma((n_ep,)),
            dma((n_ep,)),
            dma((n_ep,)),
            dma((n_rep,)),
            dma((n_rep,)),
            dma((n_rep, chunks)),
            dma((n_rep, chunks)),
            dma((3,)),
        ],
        compiler_params=pltpu.CompilerParams(
            collective_id=0, has_side_effects=True, vmem_limit_bytes=67043328
        ),
    )(
        out_grad,
        hidden.reshape(routes, inner),
        expert_ids,
        gates,
        weights[0],
        row_moment.reshape(1, own_rows),
        col_moment.reshape(1, width),
    )

    return (
        hidden_grad.reshape(tok, top, inner),
        update[None],
        row_new.reshape(1, own_rows),
        col_new.reshape(1, 1, width),
    )


def solution(mesh):
    return jax.shard_map(
        local,
        mesh=mesh,
        in_specs=(
            P(("ep", "rep"), None),
            P(("ep", "rep"), None, None),
            P(("ep", "rep"), None),
            P(("ep", "rep"), None),
            P("ep", "rep", None),
            P("ep", "rep"),
            P("ep", "rep", None),
        ),
        out_specs=(
            P(("ep", "rep"), None, None),
            P("ep", "rep", None),
            P("ep", "rep"),
            P("ep", "rep", None),
        ),
        check_vma=False,
    )
```

```python
import functools

import jax
import jax.numpy as jnp
from jax import lax
from jax.experimental import pallas as pl
from jax.experimental.pallas import tpu as pltpu
from jax.sharding import PartitionSpec as P

decay_rate = 0.9
epsilon = 1e-06
MESH = pl.DeviceIdType.MESH


def up_to(value, step):
    return -(-value // step) * step


def kernel(
    dims,
    og_ref,
    hidden_ref,
    ids_ref,
    gates_ref,
    w_ref,
    rowm_ref,
    colm_ref,
    returned_ref,
    out_ref,
    update_ref,
    rown_ref,
    coln_ref,
    og_all,
    hid,
    slot,
    table,
    place_all,
    hsend,
    hrecv,
    rows,
    igbuf,
    wfull,
    parts,
    grad,
    og_recv,
    up_sem,
    down_sem,
    y_sem,
    core_sem,
    pl_send,
    pl_recv,
    h_send,
    h_recv,
    r_send,
    r_recv,
    w_send,
    w_recv,
    g_send,
    g_recv,
    l_sem,
):
    n_ep, n_rep, outer, sent, cap, chunks = dims
    tok, width = og_ref.shape
    routes, inner = hidden_ref.shape
    top = routes // tok
    own_rows = inner // n_rep
    wide = width // chunks
    term = wfull
    me = lax.axis_index("ep")
    rep = lax.axis_index("rep")
    z, y, c = me // 4, (me // 2) % 2, me % 2
    y_dev = z * 4 + (1 - y) * 2 + c
    c_dev = z * 4 + y * 2 + (1 - c)
    way = 1 - 2 * (z // (outer // 2))

    barrier = pltpu.get_barrier_semaphore()
    for d in range(1, n_ep):
        pl.semaphore_signal(
            barrier, inc=1, device_id={"ep": lax.rem(me + d, n_ep)}, device_id_type=MESH
        )
    for d in range(1, n_rep):
        pl.semaphore_signal(
            barrier, inc=1, device_id={"rep": lax.rem(rep + d, n_rep)}, device_id_type=MESH
        )
    pl.semaphore_wait(barrier, n_ep - 1 + n_rep - 1)

    def remote(src, dst, send, recv, **where):
        return pltpu.make_async_remote_copy(
            src_ref=src, dst_ref=dst, send_sem=send, recv_sem=recv,
            device_id=where, device_id_type=MESH,
        )

    def og_copy(block, send, to, own):
        src = og_ref if own else og_all.at[block]
        return remote(src, og_all.at[block], send, og_recv.at[block], ep=to)

    def og_wait(block):
        remote(og_all.at[block], og_all.at[block], up_sem.at[0], og_recv.at[block], ep=me).wait_recv()

    def fan(zs, k, act):
        block = zs * 4 + y * 2 + c
        act(og_copy(block, y_sem.at[zs], y_dev, k == 0))
        act(og_copy(block, core_sem.at[zs * 2], c_dev, k == 0))

    def rise(zs, k, act):
        block = zs * 4 + y * 2 + c

        @pl.when(z + 1 < outer)
        def _():
            act(og_copy(block, up_sem.at[zs], me + 4, k == 0))

    def sink(zs, k, act):
        block = zs * 4 + y * 2 + c

        @pl.when(z > 0)
        def _():
            act(og_copy(block, down_sem.at[zs], me - 4, k == 0))

    def cross(zs, act):
        block = zs * 4 + (1 - y) * 2 + c
        act(og_copy(block, core_sem.at[zs * 2 + 1], c_dev, False))

    start = lambda copy: copy.start()
    finish = lambda copy: copy.wait_send()

    def own_sends(act):
        rise(z, 0, act)
        sink(z, 0, act)
        fan(z, 0, act)

    def forward(k, act, arrive):
        low, high = z - k, z + k

        @pl.when(low >= 0)
        def _():
            if arrive:
                og_wait(low * 4 + y * 2 + c)
            rise(low, k, act)
            fan(low, k, act)

        @pl.when(high < outer)
        def _():
            if arrive:
                og_wait(high * 4 + y * 2 + c)
            sink(high, k, act)
            fan(high, k, act)

    def crossing(k, act, arrive):
        for zs, ok in ((z - k, z - k >= 0), (z + k, z + k < outer))[: 1 if k == 0 else 2]:

            @pl.when(ok)
            def _():
                if arrive:
                    og_wait(zs * 4 + (1 - y) * 2 + c)
                cross(zs, act)

    own_sends(start)
    own_og = pltpu.make_async_copy(og_ref, og_all.at[me], l_sem.at[0])
    own_w = pltpu.make_async_copy(w_ref, wfull.at[rep], l_sem.at[1])
    own_hidden = pltpu.make_async_copy(hidden_ref, hid, l_sem.at[2])
    own_hidden.start()
    own_og.start()
    own_w.start()
    w_copies = []
    for d in range(1, n_rep):
        q = lax.rem(rep + d, n_rep)
        w_copies.append(remote(w_ref, wfull.at[rep], w_send.at[d], w_recv.at[rep], rep=q))
        w_copies[-1].start()

    experts = lax.broadcasted_iota(jnp.int32, (n_ep, tok), 0)
    chosen = jnp.zeros(experts.shape, jnp.float32)
    gate = jnp.zeros(experts.shape, jnp.float32)
    for k in range(top):
        named = experts == ids_ref[k : k + 1, :]
        chosen = jnp.where(named, 1.0, chosen)
        gate = jnp.where(named, gates_ref[k : k + 1, :], gate)
    row_i = lax.broadcasted_iota(jnp.int32, (tok, tok), 0)
    col_i = lax.broadcasted_iota(jnp.int32, (tok, tok), 1)
    earlier = jnp.where(row_i < col_i, 1.0, 0.0).astype(jnp.bfloat16)
    rank = lax.dot_general(
        chosen.astype(jnp.bfloat16), earlier, (((1,), (0,)), ((), ())),
        preferred_element_type=jnp.float32,
    )
    place = jnp.where(chosen > 0.5, rank, -1.0)
    first_row = lax.broadcasted_iota(jnp.int32, (n_ep, 8, tok), 1) == 0
    table[...] = jnp.where(first_row, place[:, None, :], gate[:, None, :])
    place_all[me] = table[me]
    if cap > sent:
        hrecv[:, sent:, :] = jnp.zeros((n_ep, cap - sent, inner), jnp.bfloat16)

    spread = jnp.where(
        lax.broadcasted_iota(jnp.int32, (tok, routes), 1) // top
        == lax.broadcasted_iota(jnp.int32, (tok, routes), 0), 1.0, 0.0,
    ).astype(jnp.bfloat16)
    named = lax.dot_general(
        ids_ref[...].astype(jnp.float32).astype(jnp.bfloat16), spread, (((1,), (0,)), ((), ())),
        preferred_element_type=jnp.float32,
    )
    turn = lax.broadcasted_iota(jnp.int32, (top, routes), 1) % top
    mine = turn == lax.broadcasted_iota(jnp.int32, (top, routes), 0)
    named = jnp.sum(jnp.where(mine, named, 0.0), axis=0, keepdims=True)
    ranks = jnp.dot(place.astype(jnp.bfloat16), spread, preferred_element_type=jnp.float32)
    number = lax.broadcasted_iota(jnp.int32, (n_ep, routes), 0).astype(jnp.float32)
    slot[...] = jnp.sum(
        jnp.where(named == number, ranks + number * cap, 0.0), axis=0, keepdims=True
    )

    def place_copy(d):
        e = lax.rem(me + d, n_ep)
        return remote(table.at[e], place_all.at[me], pl_send.at[d], pl_recv.at[me], ep=e)

    @pl.loop(1, n_ep)
    def _(d):
        place_copy(d).start()

    def h_copy(e):
        return remote(hsend.at[e, pl.ds(0, sent)], hrecv.at[me, pl.ds(0, sent)], h_send.at[e], h_recv.at[me], ep=e)

    def r_copy(s):
        return remote(igbuf.at[s, pl.ds(0, sent)], returned_ref.at[me], r_send.at[s], r_recv.at[me], ep=s)

    def plane(k):
        return lax.rem(z + way * k + outer, outer)

    def slot_pick(first):
        ids = lax.broadcasted_iota(jnp.int32, (4 * cap, routes), 0) + first * cap
        return jnp.where(ids.astype(jnp.float32) == slot[...], 1.0, 0.0).astype(jnp.bfloat16)

    def hidden_group(k):
        first = plane(k) * 4
        got = jnp.dot(slot_pick(first), hid[...], preferred_element_type=jnp.float32)
        hsend[pl.ds(first, 4)] = got.astype(jnp.bfloat16).reshape(4, cap, inner)

        @pl.loop(0, 4)
        def _(i):
            e = first + i

            @pl.when(e != me)
            def _():
                h_copy(e).start()

            @pl.when(e == me)
            def _():
                hrecv[me] = hsend[me]

    own_hidden.wait()
    hidden_group(0)
    for k in range(1, outer):
        forward(k, start, True)
        hidden_group(k)
        crossing(k - 1, start, True)

    for d in range(1, n_rep):
        q = lax.rem(rep + d, n_rep)
        remote(w_ref, wfull.at[q], w_send.at[d], w_recv.at[q], rep=q).wait_recv()

    @pl.loop(1, n_ep)
    def _(d):
        s = lax.rem(me + d, n_ep)
        remote(table.at[s], place_all.at[s], pl_send.at[d], pl_recv.at[s], ep=s).wait_recv()

    own_og.wait()
    own_w.wait()

    @pl.loop(0, outer)
    def _(k):
        @pl.when(k == outer - 1)
        def _():
            crossing(outer - 1, start, True)

        first = plane(k) * 4
        og_wait(first + 1 - c)
        og_wait(first + 3 - c)

        @pl.loop(0, 4)
        def _(i):
            s = first + i
            info = place_all[s]
            ids = lax.broadcasted_iota(jnp.int32, (cap, tok), 0).astype(jnp.float32)
            pick = jnp.where(ids == info[0:1, :], 1.0, 0.0)
            factor = jnp.sum(pick * info[1:2, :], axis=1, keepdims=True)
            got = factor * jnp.dot(
                pick.astype(jnp.bfloat16), og_all[s], preferred_element_type=jnp.float32
            )
            rows[pl.ds(pl.multiple_of(s * cap, 16), cap), :] = got.astype(jnp.bfloat16)

        here = rows[pl.ds(pl.multiple_of(first * cap, 16), 4 * cap), :]
        back = lax.dot_general(
            here,
            wfull[...].reshape(inner, width),
            (((1,), (1,)), ((), ())),
            preferred_element_type=jnp.float32,
        )
        igbuf[pl.ds(first, 4)] = back.astype(jnp.bfloat16).reshape(4, cap, inner)

        @pl.loop(0, 4)
        def _(i):
            s = first + i

            @pl.when(s != me)
            def _():
                r_copy(s).start()

    own = pltpu.make_async_copy(igbuf.at[me, pl.ds(0, sent)], returned_ref.at[me], r_recv.at[me])
    own.start()

    @pl.loop(1, n_ep)
    def _(d):
        s = lax.rem(me + d, n_ep)
        remote(hsend.at[s, pl.ds(0, sent)], hrecv.at[s, pl.ds(0, sent)], h_send.at[s], h_recv.at[s], ep=s).wait_recv()

    def g_copy(d, j, q, slot):
        cols = pl.ds(j * wide, wide)
        return remote(
            term.at[q, :, cols], parts.at[slot, :, cols],
            g_send.at[d, j], g_recv.at[slot, j], rep=q,
        )

    left = hrecv[...].reshape(n_ep * cap, inner)
    for j in range(chunks):
        cols = pl.ds(j * wide, wide)
        got = lax.dot_general(
            left, rows[:, cols], (((0,), (0,)), ((), ())), preferred_element_type=jnp.float32
        )
        term[:, :, cols] = got.astype(jnp.bfloat16).reshape(n_rep, own_rows, wide)
        for d in range(1, n_rep):
            g_copy(d, j, lax.rem(rep + d, n_rep), rep).start()

    def back_copy(first):
        return pltpu.make_async_copy(
            returned_ref.at[pl.ds(first, 4)], hsend.at[pl.ds(first, 4), pl.ds(0, sent)], l_sem.at[0]
        )

    def collect(k):
        first = plane(k) * 4

        @pl.loop(0, 4)
        def _(i):
            s = first + i

            @pl.when(s != me)
            def _():
                h_copy(s).wait_send()
                remote(
                    igbuf.at[s, pl.ds(0, sent)], returned_ref.at[s], r_send.at[s], r_recv.at[s], ep=s
                ).wait_recv()

        back_copy(first).start()
        back_copy(first).wait()
        got = lax.dot_general(
            slot_pick(first),
            hsend[pl.ds(first, 4)].reshape(4 * cap, inner),
            (((0,), (0,)), ((), ())),
            preferred_element_type=jnp.float32,
        ).astype(jnp.bfloat16)
        out_ref[...] = got if k == 0 else out_ref[...] + got

    own.wait()
    for k in range(outer - 1):
        collect(k)

    total = jnp.zeros((own_rows, 1), jnp.float32)
    for j in range(chunks):
        cols = pl.ds(j * wide, wide)
        part = term[rep, :, cols].astype(jnp.float32)
        for d in range(1, n_rep):
            q = lax.rem(rep + d, n_rep)
            g_copy(d, j, q, q).wait_recv()
            part = part + parts[q, :, cols].astype(jnp.float32)
        grad[:, cols] = part
        square = part * part
        total = total + jnp.sum(square, axis=1, keepdims=True)
        coln_ref[:, cols] = decay_rate * colm_ref[:, cols] + (1.0 - decay_rate) * (
            jnp.sum(square, axis=0, keepdims=True) / own_rows + epsilon
        )
    diagonal = lax.broadcasted_iota(jnp.int32, (own_rows, own_rows), 0) == (
        lax.broadcasted_iota(jnp.int32, (own_rows, own_rows), 1)
    )
    rowm = jnp.sum(jnp.where(diagonal, rowm_ref[...], 0.0), axis=1, keepdims=True)
    row_new = decay_rate * rowm + (1.0 - decay_rate) * (total / width + epsilon)
    rown_ref[...] = jnp.sum(jnp.where(diagonal, row_new, 0.0), axis=0, keepdims=True)
    mean = jnp.sum(row_new, axis=0, keepdims=True) / own_rows
    for j in range(chunks):
        cols = pl.ds(j * wide, wide)
        second = row_new * coln_ref[:, cols] / mean
        update_ref[:, cols] = (grad[:, cols] * lax.rsqrt(second)).astype(jnp.bfloat16)

    collect(outer - 1)

    @pl.loop(1, n_ep)
    def _(d):
        s = lax.rem(me + d, n_ep)
        place_copy(d).wait_send()
        r_copy(s).wait_send()

    own_sends(finish)
    for k in range(1, outer):
        forward(k, finish, False)
        crossing(k - 1, finish, False)
    crossing(outer - 1, finish, False)
    for copy in w_copies:
        copy.wait_send()
    for j in range(chunks):
        for d in range(1, n_rep):
            g_copy(d, j, lax.rem(rep + d, n_rep), rep).wait_send()


def local(out_grad, hidden, expert_ids, gates, weights, row_moment, col_moment):
    tok, top = expert_ids.shape
    width = out_grad.shape[1]
    inner = hidden.shape[2]
    n_ep, n_rep = lax.axis_size("ep"), lax.axis_size("rep")
    capacity = max(2, tok * top * 9 // (8 * n_ep))
    sent, cap = up_to(capacity, 8), up_to(capacity, 16)
    outer = n_ep // 4
    own_rows = inner // n_rep
    routes = tok * top
    chunks = 4

    vmem = pl.BlockSpec(memory_space=pltpu.VMEM)
    anywhere = pl.BlockSpec(memory_space=pl.ANY)
    dma = pltpu.SemaphoreType.DMA
    _, hidden_grad, update, row_new, col_new = pl.pallas_call(
        functools.partial(kernel, (n_ep, n_rep, outer, sent, cap, chunks)),
        out_shape=(
            jax.ShapeDtypeStruct((n_ep, sent, inner), jnp.bfloat16),
            jax.ShapeDtypeStruct((routes, inner), jnp.bfloat16),
            jax.ShapeDtypeStruct((own_rows, width), jnp.bfloat16),
            jax.ShapeDtypeStruct((1, own_rows), jnp.float32),
            jax.ShapeDtypeStruct((1, width), jnp.float32),
        ),
        in_specs=[anywhere, anywhere, vmem, vmem, anywhere, vmem, vmem],
        out_specs=(anywhere, vmem, vmem, vmem, vmem),
        scratch_shapes=[
            pltpu.VMEM((n_ep, tok, width), jnp.bfloat16),
            pltpu.VMEM((routes, inner), jnp.bfloat16),
            pltpu.VMEM((1, routes), jnp.float32),
            pltpu.VMEM((n_ep, 8, tok), jnp.float32),
            pltpu.VMEM((n_ep, 8, tok), jnp.float32),
            pltpu.VMEM((n_ep, cap, inner), jnp.bfloat16),
            pltpu.VMEM((n_ep, cap, inner), jnp.bfloat16),
            pltpu.VMEM((n_ep * cap, width), jnp.bfloat16),
            pltpu.VMEM((n_ep, cap, inner), jnp.bfloat16),
            pltpu.VMEM((n_rep, own_rows, width), jnp.bfloat16),
            pltpu.VMEM((n_rep, own_rows, width), jnp.bfloat16),
            pltpu.VMEM((own_rows, width), jnp.float32),
            dma((n_ep,)),
            dma((outer,)),
            dma((outer,)),
            dma((outer,)),
            dma((2 * outer,)),
            dma((n_ep,)),
            dma((n_ep,)),
            dma((n_ep,)),
            dma((n_ep,)),
            dma((n_ep,)),
            dma((n_ep,)),
            dma((n_rep,)),
            dma((n_rep,)),
            dma((n_rep, chunks)),
            dma((n_rep, chunks)),
            dma((3,)),
        ],
        compiler_params=pltpu.CompilerParams(
            collective_id=0, has_side_effects=True, vmem_limit_bytes=67043328
        ),
    )(
        out_grad,
        hidden.reshape(routes, inner),
        expert_ids.T,
        gates.T,
        weights[0],
        row_moment.reshape(1, own_rows),
        col_moment.reshape(1, width),
    )

    return (
        hidden_grad.reshape(tok, top, inner),
        update[None],
        row_new.reshape(1, own_rows),
        col_new.reshape(1, 1, width),
    )


def solution(mesh):
    return jax.shard_map(
        local,
        mesh=mesh,
        in_specs=(
            P(("ep", "rep"), None),
            P(("ep", "rep"), None, None),
            P(("ep", "rep"), None),
            P(("ep", "rep"), None),
            P("ep", "rep", None),
            P("ep", "rep"),
            P("ep", "rep", None),
        ),
        out_specs=(
            P(("ep", "rep"), None, None),
            P("ep", "rep", None),
            P("ep", "rep"),
            P("ep", "rep", None),
        ),
        check_vma=False,
    )
```
